32 devices in a mesh: gx: 4 (over y, x), gy: 2 (over core), gz: 4 (over z).
Axes of the slice: x: 2, y: 2, z: 4, core: 2. Of those that a mesh axis runs over, the one named last changes fastest.
Arguments:
- state: float32 [5, 16, 32, 512], P(None, 'gx', 'gy', 'gz'), may hold values from -2 to 8, as said below
- volume: float32 [16, 32, 512], P('gx', 'gy', 'gz'), may hold values from 0 to 1, as said below
- apertures: float32 [3, 16, 32, 512], P(None, 'gx', 'gy', 'gz'), may hold values from 0 to 1, as said below
- flags: int32 [16, 32, 512], P('gx', 'gy', 'gz'), may hold values from 0 to 2, as said below
Outputs:
- step_rate: float32 [5, 16, 32, 512], P(None, 'gx', 'gy', 'gz')
The draws below stay inside these ranges and needn't reach their ends.
Inputs may be any that keep to these rules, and one draw needn't show every extreme that they name: `flags`: in every column of cells the lowest cells are solid (flag 2), one cut cell (flag 1) follows, fluid cells (flag 0) lie above; the cut cell lies between layers 8 and 23. `volume`: 0 in solid cells, between 0.05 and 0.95 in cut cells, 1 in fluid cells; equal to the height of fluid in the cell over a terrain surface. `apertures`: the open part of each face below which the terrain surface lies; lower z faces of solid and cut cells are closed. `state`: density between 0.5 and 2, velocity components between -1 and 1, pressure between 0.5 and 2.
All inputs are finite; a program needn't handle non-finite values.
Results may differ from the reference program's by a relative error of at most 0.0003.
Values sent between devices are 32-bit elements; how exact they have to be, the bound alone decides.
A program may use at most 64 MiB of HBM per device.

```python
import jax
import jax.numpy as jnp
from jax import lax

NF = 5
CUTZ = 32
CX = 4
NX = 16
NY = 32
NZ = 512
N_GX = 4


def terrain(key):
    base_key = jax.random.fold_in(key, 17)
    heights = jax.random.randint(jax.random.fold_in(base_key, 1), (NX, NY), CUTZ // 4, 3 * CUTZ // 4)
    fraction = jax.random.uniform(jax.random.fold_in(base_key, 2), (NX, NY), jnp.float32, 0.05, 0.95)
    return (heights, fraction)


def surface_top(key):
    heights, fraction = terrain(key)
    return (heights, heights.astype(jnp.float32) + 1.0 - fraction)


def draw_volume(key, part):
    heights, surface = surface_top(key)
    levels = jnp.arange(NZ, dtype=jnp.float32)
    return jnp.clip(levels[None, None, :] + 1.0 - surface[:, :, None], 0.0, 1.0)


def draw_apertures(key, part):
    heights, surface = surface_top(key)
    levels = jnp.arange(NZ, dtype=jnp.float32)
    side_x = jnp.maximum(surface, jnp.roll(surface, 1, axis=0))
    side_y = jnp.maximum(surface, jnp.roll(surface, 1, axis=1))
    open_x = jnp.clip(levels[None, None, :] + 1.0 - side_x[:, :, None], 0.0, 1.0)
    open_y = jnp.clip(levels[None, None, :] + 1.0 - side_y[:, :, None], 0.0, 1.0)
    int_levels = jnp.arange(NZ, dtype=jnp.int32)
    open_z = (int_levels[None, None, :] > heights[:, :, None]).astype(jnp.float32)
    return jnp.stack([open_x, open_y, open_z])


def draw_flags(key, part):
    heights, fraction = terrain(key)
    levels = jnp.arange(NZ, dtype=jnp.int32)[None, None, :]
    column = heights[:, :, None]
    return jnp.where(levels < column, 2, jnp.where(levels == column, 1, 0)).astype(jnp.int32)


def draw_state(key, part):
    state_key = jax.random.fold_in(key, 5)
    density = jax.random.uniform(jax.random.fold_in(state_key, 1), (NX, NY, NZ), jnp.float32, 0.5, 2.0)
    velocity = jax.random.uniform(jax.random.fold_in(state_key, 2), (3, NX, NY, NZ), jnp.float32, -1.0, 1.0)
    pressures = jax.random.uniform(jax.random.fold_in(state_key, 3), (NX, NY, NZ), jnp.float32, 0.5, 2.0)
    energy = pressures / 0.4 + 0.5 * density * jnp.sum(velocity * velocity, axis=0)
    return jnp.concatenate([density[None], density[None] * velocity, energy[None]], axis=0)


def setup_inputs(seed: int = 0) -> dict:
    key_of = jax.random.split(jax.random.key(seed), 5)
    return {
        "state": draw_state(jax.random.fold_in(key_of[4], 71), 0),
        "volume": draw_volume(jax.random.fold_in(key_of[4], 71), 0),
        "apertures": draw_apertures(jax.random.fold_in(key_of[4], 71), 0),
        "flags": draw_flags(jax.random.fold_in(key_of[4], 71), 0),
    }


GAMMA_LESS = 0.4
DISSIPATION = 4.0
TIME_STEP = 0.02
VOLUME_FLOOR = 0.5


def minmod(lower, upper):
    return 0.5 * (jnp.sign(lower) + jnp.sign(upper)) * jnp.minimum(jnp.abs(lower), jnp.abs(upper))


def pressure(cell_state):
    kinetic = cell_state[1] * cell_state[1] + cell_state[2] * cell_state[2] + cell_state[3] * cell_state[3]
    return GAMMA_LESS * (cell_state[4] - 0.5 * kinetic / cell_state[0])


def physical_flux(cell_state, direction):
    velocity = cell_state[direction] / cell_state[0]
    pressures = pressure(cell_state)
    components = [cell_state[direction], cell_state[1] * velocity, cell_state[2] * velocity,
                  cell_state[3] * velocity, (cell_state[4] + pressures) * velocity]
    components[direction] = components[direction] + pressures
    return jnp.stack(components)


def trim_axis(array, dimension, offset, extent):
    return lax.slice_in_dim(array, offset, offset + extent, axis=dimension)


def face_flux(column_part, direction, margin, extent):
    length = column_part.shape[direction]
    differences = trim_axis(column_part, direction, 1, length - 1) - trim_axis(column_part, direction, 0, length - 1)
    slopes = minmod(trim_axis(differences, direction, 0, length - 2), trim_axis(differences, direction, 1, length - 2))
    left_state = trim_axis(column_part, direction, margin - 1, extent + 1) + 0.5 * trim_axis(slopes, direction, margin - 2, extent + 1)
    right_state = trim_axis(column_part, direction, margin, extent + 1) - 0.5 * trim_axis(slopes, direction, margin - 1, extent + 1)
    average = 0.5 * (physical_flux(left_state, direction) + physical_flux(right_state, direction))
    return average - 0.5 * DISSIPATION * (right_state - left_state)


def section_rate(padded, margin, openings, open_margin, volume, fluid_mask):
    extents = [padded.shape[dimension] - 2 * margin for dimension in (1, 2, 3)]
    centre = padded
    for dimension in (1, 2, 3):
        centre = trim_axis(centre, dimension, margin, extents[dimension - 1])
    pressures = pressure(centre)
    divergence = jnp.zeros_like(centre)
    pushes = []
    for direction in (1, 2, 3):
        column_part = padded
        face_open = openings
        for other_axis in (1, 2, 3):
            if other_axis != direction:
                column_part = trim_axis(column_part, other_axis, margin, extents[other_axis - 1])
                face_open = trim_axis(face_open, other_axis, open_margin, extents[other_axis - 1])
        extent = extents[direction - 1]
        face_open = trim_axis(face_open[direction - 1], direction - 1, open_margin, extent + 1)
        fluxes = face_flux(column_part, direction, margin, extent) * face_open[None]
        divergence = divergence + trim_axis(fluxes, direction, 1, extent) - trim_axis(fluxes, direction, 0, extent)
        pushes.append(pressures * (trim_axis(face_open, direction - 1, 1, extent) - trim_axis(face_open, direction - 1, 0, extent)))
    wall_force = jnp.stack([jnp.zeros_like(pressures)] + pushes + [jnp.zeros_like(pressures)])
    return (wall_force - divergence) / jnp.maximum(volume, VOLUME_FLOOR) * fluid_mask


def redistribute(rates, volume, excess):
    moved_sum = jnp.sum(excess[None] * rates, axis=3)
    weight = jnp.sum(volume, axis=2)
    return (1.0 - excess[None]) * rates + volume[None] * (moved_sum / weight[None])[..., None]


def full_rate(current, apertures, volume, fluid_mask, excess):
    padded = jnp.pad(current, ((0, 0), (2, 2), (2, 2), (2, 2)), mode="wrap")
    openings = jnp.pad(apertures, ((0, 0), (1, 1), (1, 1), (1, 1)), mode="wrap")

    def block_rate(block_index):
        offset = block_index * CX
        cell_block = lax.dynamic_slice_in_dim(padded, offset, CX + 4, axis=1)
        open_block = lax.dynamic_slice_in_dim(openings, offset, CX + 2, axis=1)
        vol_block = lax.dynamic_slice_in_dim(volume, offset, CX, axis=0)
        fluid_block = lax.dynamic_slice_in_dim(fluid_mask, offset, CX, axis=0)
        excess_block = lax.dynamic_slice_in_dim(excess, offset, CX, axis=0)
        rates = section_rate(cell_block, 2, open_block, 1, vol_block, fluid_block)
        spread = redistribute(rates[..., :CUTZ], vol_block[..., :CUTZ], excess_block[..., :CUTZ])
        return jnp.concatenate([spread, rates[..., CUTZ:]], axis=3)

    block_rates = lax.map(block_rate, jnp.arange(N_GX, dtype=jnp.int32))
    return jnp.moveaxis(block_rates, 0, 1).reshape(NF, NX, NY, NZ)


def reference(state, volume, apertures, flags):
    fluid_mask = (flags != 2).astype(jnp.float32)
    excess = (1.0 - volume) * (flags == 1).astype(jnp.float32)
    first_rate = full_rate(state, apertures, volume, fluid_mask, excess)
    middle = state + TIME_STEP * first_rate
    second = full_rate(middle, apertures, volume, fluid_mask, excess)
    return 0.5 * (first_rate + second)
```

```python
import jax
import jax.numpy as jnp
from jax import lax
from jax.experimental import pallas as pl
from jax.experimental.pallas import tpu as pltpu
from jax.sharding import PartitionSpec as P

CUTZ = 32
NF = 5
GAMMA_LESS = 0.4
DISSIPATION = 4.0
TIME_STEP = 0.02
VOLUME_FLOOR = 0.5
PAD = 8

MESH = pl.DeviceIdType.MESH


def minmod(a, b):
    return jnp.maximum(jnp.minimum(a, b), 0.0) + jnp.minimum(jnp.maximum(a, b), 0.0)


def pressure_of(w, inverse):
    kinetic = w[1] * w[1] + w[2] * w[2] + w[3] * w[3]
    return GAMMA_LESS * (w[4] - 0.5 * kinetic * inverse)


def flux(w, d):
    inverse = 1.0 / w[0]
    u = w[d] * inverse
    p = pressure_of(w, inverse)
    out = [w[d], w[1] * u, w[2] * u, w[3] * u, (w[4] + p) * u]
    out[d] = out[d] + p
    return out


def face(left, right, d, half_open):
    fl, fr = flux(left, d), flux(right, d)
    return [
        ((fl[f] + fr[f]) + DISSIPATION * (left[f] - right[f])) * half_open for f in range(NF)
    ]


def kernel(
    state, volume, apertures, flags, out,
    buf1, buf2, ox, oy, oz, vol, flg, pk, rec_low, rec_high, gfix, sfix, afix, acc,
    first, scale, keep, gain, local_sem, send_sem, recv_sem,
):
    _, X, Y, Z = state.shape
    F4 = 4 * X
    me = [lax.axis_index(a) for a in ("gx", "gy", "gz")]
    size = [lax.axis_size(a) for a in ("gx", "gy", "gz")]
    up = [{a: lax.rem(me[i] + 1, size[i])} for i, a in enumerate(("gx", "gy", "gz"))]
    down = [{a: lax.rem(me[i] + size[i] - 1, size[i])} for i, a in enumerate(("gx", "gy", "gz"))]

    rows = pl.ds(PAD, Y)
    loads = [
        (state, buf1.at[:, pl.ds(2, X), rows, :]),
        (apertures.at[0], ox.at[pl.ds(0, X)]),
        (apertures.at[1], oy.at[:, pl.ds(0, Y), :]),
        (apertures.at[2], oz),
        (volume, vol),
        (flags, flg),
    ]
    loads = [pltpu.make_async_copy(s, d, local_sem.at[i]) for i, (s, d) in enumerate(loads)]
    for load in loads:
        load.start()

    barrier = pltpu.get_barrier_semaphore()
    for i in range(3):
        pl.semaphore_signal(barrier, inc=1, device_id=up[i], device_id_type=MESH)
        pl.semaphore_signal(barrier, inc=1, device_id=down[i], device_id_type=MESH)
    pl.semaphore_wait(barrier, 6)

    def remote(src, dst, slot, target):
        return pltpu.make_async_remote_copy(
            src_ref=src, dst_ref=dst, send_sem=send_sem.at[slot], recv_sem=recv_sem.at[slot],
            device_id=target, device_id_type=MESH,
        )

    def x_copies(src, x0, r, buf, slot):
        own = lambda lo: src.at[:, pl.ds(x0 + lo, 2), r, :]
        return (
            remote(own(0), buf.at[:, pl.ds(X + 2, 2), rows, :], slot, down[0]),
            remote(own(X - 2), buf.at[:, pl.ds(0, 2), rows, :], slot + 1, up[0]),
        )

    def y_copies(src, x0, y0, buf, slot):
        mid = pl.ds(x0, X)
        return (
            remote(src.at[:, mid, pl.ds(y0, 2), :],
                   buf.at[:, pl.ds(2, X), pl.ds(PAD + Y, 2), :], slot, down[1]),
            remote(src.at[:, mid, pl.ds(y0 + Y - 2, 2), :],
                   buf.at[:, pl.ds(2, X), pl.ds(PAD - 2, 2), :], slot + 1, up[1]),
        )

    def z_copies(stage, slot):
        return (
            remote(pk.at[stage], rec_high.at[stage], slot, down[2]),
            remote(pk.at[stage], rec_low.at[stage], slot + 1, up[2]),
        )

    xs1 = x_copies(state, 0, pl.ds(0, Y), buf1, 0)
    ys1 = y_copies(state, 0, 0, buf1, 2)
    ax = remote(apertures.at[0, pl.ds(0, 1)], ox.at[pl.ds(X, 1)], 4, down[0])
    ay = remote(apertures.at[1, :, pl.ds(0, 1), :], oy.at[:, pl.ds(Y, 1), :], 5, down[1])
    for c in xs1 + ys1 + (ax, ay):
        c.start()
    for load in loads:
        load.wait()

    lane = lax.broadcasted_iota(jnp.int32, (Y, Z), 1)
    quad = lax.rem(lane, 4)

    def pack(buf, stage):
        packed = jnp.zeros((Y, Z), jnp.float32)
        for f in range(NF + 1):
            for x in range(X):
                base = f * F4 + 4 * x
                value = buf[f, x + 2, PAD:PAD + Y, :] if f < NF else oz[x]
                inside = (lane >= base) & (lane < base + 4)
                packed = jnp.where(inside, pltpu.roll(value, base + 2, 1), packed)
        pk[stage] = packed

    pack(buf1, 0)
    zs1 = z_copies(0, 6)
    for c in zs1:
        c.start()

    limit = jnp.where(me[2] == 0, CUTZ, 0)
    for x in range(X):
        v = vol[x]
        fl = flg[x]
        weight = jnp.sum(jnp.where(lane < CUTZ, v, 0.0), axis=1, keepdims=True)
        excess = jnp.where((fl == 1) & (lane < limit), 1.0 - v, 0.0)
        scale[x] = jnp.where(fl != 2, 1.0 / jnp.maximum(v, VOLUME_FLOOR), 0.0)
        keep[x] = excess
        gain[x] = jnp.where(lane < limit, v / weight, 0.0)

    def boundary_z(stage):
        own, low, high = pk[stage], rec_low[stage], rec_high[stage]
        lefts, rights, slopes = [], [], []
        for c in (jnp.where(quad < 2, own, high), jnp.where(quad < 2, low, own)):
            d = c - pltpu.roll(c, 1, 1)
            s = minmod(d, pltpu.roll(d, Z - 1, 1))
            slopes.append(s)
            lefts.append(c + 0.5 * s)
            rights.append(c - 0.5 * s)
        top = quad == 0
        left = jnp.where(top, pltpu.roll(lefts[0], Z - 1, 1), lefts[1])
        right = jnp.where(
            top, pltpu.roll(rights[0], Z - 2, 1), pltpu.roll(rights[1], Z - 1, 1)
        )
        sfix[...] = jnp.where(
            top, pltpu.roll(slopes[0], Z - 1, 1), pltpu.roll(slopes[1], Z - 1, 1)
        )
        opening = jnp.where(
            top, pltpu.roll(high, Z - 2, 1), pltpu.roll(own, Z - 1, 1)
        )
        ls = [pltpu.roll(left, Z - f * F4, 1) if f else left for f in range(NF)]
        rs = [pltpu.roll(right, Z - f * F4, 1) if f else right for f in range(NF)]
        opening = pltpu.roll(opening, Z - NF * F4, 1)
        live = lane < F4
        ls = [jnp.where(live & (quad < 2), w, 1.0) for w in ls]
        rs = [jnp.where(live & (quad < 2), w, 1.0) for w in rs]
        g = face(ls, rs, 3, 0.5 * opening)
        for f in range(NF):
            gfix[f] = g[f]
        afix[...] = opening

    def yz_part(x, buf):
        v = [buf[f, x + 2, PAD:PAD + Y, :] for f in range(NF)]
        p = pressure_of(v, 1.0 / v[0])
        a = oz[x]
        shift = Z - (4 * x + 1)
        sl = []
        for f in range(NF):
            d = v[f] - pltpu.roll(v[f], 1, 1)
            s = minmod(d, pltpu.roll(d, Z - 1, 1))
            fix = pltpu.roll(sfix[...], lax.rem(2 * Z - (f * F4 + 4 * x + 1), Z), 1)
            sl.append(0.5 * jnp.where((lane == 0) | (lane == Z - 1), fix, s))
        left = [pltpu.roll(v[f] + sl[f], 1, 1) for f in range(NF)]
        right = [v[f] - sl[f] for f in range(NF)]
        g = face(left, right, 3, 0.5 * a)
        div = []
        for f in range(NF):
            fix = pltpu.roll(gfix[f], shift, 1)
            low = jnp.where(lane == 0, fix, g[f])
            high = jnp.where(lane == Z - 1, fix, pltpu.roll(g[f], Z - 1, 1))
            div.append(high - low)
        a_high = jnp.where(
            lane == Z - 1, pltpu.roll(afix[...], shift, 1), pltpu.roll(a, Z - 1, 1)
        )
        div[3] = div[3] - p * (a_high - a)
        E = Y + 8
        left, right = [], []
        for f in range(NF):
            c = buf[f, x + 2, PAD - 1:PAD - 1 + E, :]
            b = buf[f, x + 2, PAD - 2:PAD - 2 + E, :]
            n = buf[f, x + 2, PAD:PAD + E, :]
            s = 0.5 * minmod(c - b, n - c)
            left.append(c + s)
            right.append(pltpu.roll(c - s, E - 1, 0))
        a = oy[x]
        g = face(left, right, 2, 0.5 * a)
        for f in range(NF):
            div[f] = div[f] + (pltpu.roll(g[f], E - 1, 0)[:Y] - g[f][:Y])
        div[2] = div[2] - p * (oy[x, 1:Y + 1, :] - oy[x, 0:Y, :])
        div[1] = div[1] - p * (ox[x + 1] - ox[x])
        for f in range(NF):
            acc[f, x] = div[f]

    def x_part(buf, finish):
        def load(f, x):
            return buf[f, x + 2, PAD:PAD + Y, :]

        def half_slope(x):
            return [
                0.5 * minmod(load(f, x) - load(f, x - 1), load(f, x + 1) - load(f, x))
                for f in range(NF)
            ]

        s = half_slope(-1)
        left = [load(f, -1) + s[f] for f in range(NF)]
        below = None
        for x in range(X + 1):
            s = half_slope(x)
            right = [load(f, x) - s[f] for f in range(NF)]
            g = face(left, right, 1, 0.5 * ox[x])
            left = [load(f, x) + s[f] for f in range(NF)]
            if x > 0:
                c = x - 1
                rates = []
                for f in range(NF):
                    base = -(acc[f, c] + (g[f] - below[f])) * scale[c]
                    moved = jnp.sum(keep[c] * base, axis=1, keepdims=True)
                    rates.append((1.0 - keep[c]) * base + gain[c] * moved)
                finish(c, rates)
            below = g

    def yz_loop(buf):
        def body(x, carry):
            yz_part(x, buf)
            return carry

        lax.fori_loop(0, X, body, 0)

    def arrive(copies):
        for c in copies:
            c.wait_recv()

    arrive(zs1 + ys1 + (ax, ay))
    boundary_z(0)
    yz_loop(buf1)
    arrive(xs1)

    xs2 = x_copies(buf2, 2, rows, buf2, 8)
    ys2 = y_copies(buf2, 2, PAD, buf2, 10)
    zs2 = z_copies(1, 12)

    def finish_first(c, rates):
        for f in range(NF):
            first[f, c] = rates[f]
            buf2[f, c + 2, PAD:PAD + Y, :] = buf1[f, c + 2, PAD:PAD + Y, :] + TIME_STEP * rates[f]
        if c == 1:
            xs2[0].start()
        if c == X - 1:
            xs2[1].start()

    x_part(buf1, finish_first)
    for c in ys2:
        c.start()
    pack(buf2, 1)
    for c in zs2:
        c.start()

    arrive(zs2 + ys2)
    boundary_z(1)
    yz_loop(buf2)
    arrive(xs2)

    def finish_second(c, rates):
        for f in range(NF):
            out[f, c] = 0.5 * (first[f, c] + rates[f])

    x_part(buf2, finish_second)
    for c in xs1 + ys1 + zs1 + (ax, ay) + xs2 + ys2 + zs2:
        c.wait_send()


def on_device(state, volume, apertures, flags):
    _, X, Y, Z = state.shape
    f32 = jnp.float32
    wide = pltpu.VMEM((NF, X + 4, Y + 2 * PAD, Z), f32)
    cells = pltpu.VMEM((X, Y, Z), f32)
    fields = pltpu.VMEM((NF, X, Y, Z), f32)
    layer = pltpu.VMEM((Y, Z), f32)
    pair = pltpu.VMEM((2, Y, Z), f32)
    return pl.pallas_call(
        kernel,
        out_shape=jax.ShapeDtypeStruct(state.shape, f32),
        in_specs=[pl.BlockSpec(memory_space=pl.ANY)] * 4,
        out_specs=pl.BlockSpec(memory_space=pltpu.VMEM),
        scratch_shapes=[
            wide, wide,
            pltpu.VMEM((X + 1, Y, Z), f32),
            pltpu.VMEM((X, Y + 8, Z), f32),
            cells, cells, pltpu.VMEM((X, Y, Z), jnp.int32),
            pair, pair, pair,
            pltpu.VMEM((NF, Y, Z), f32), layer, layer,
            fields, fields, cells, cells, cells,
            pltpu.SemaphoreType.DMA((6,)),
            pltpu.SemaphoreType.DMA((14,)),
            pltpu.SemaphoreType.DMA((14,)),
        ],
        compiler_params=pltpu.CompilerParams(collective_id=0, has_side_effects=True),
    )(state, volume, apertures, flags)


def solution(mesh):
    in_specs = (
        P(None, "gx", "gy", "gz"),
        P("gx", "gy", "gz"),
        P(None, "gx", "gy", "gz"),
        P("gx", "gy", "gz"),
    )
    return jax.shard_map(
        on_device, mesh=mesh, in_specs=in_specs, out_specs=P(None, "gx", "gy", "gz"),
        check_vma=False,
    )
```

```python
import jax
import jax.numpy as jnp
from jax import lax
from jax.experimental import pallas as pl
from jax.experimental.pallas import tpu as pltpu
from jax.sharding import PartitionSpec as P

CUTZ = 32
NF = 5
GAMMA_LESS = 0.4
DISSIPATION = 4.0
TIME_STEP = 0.02
VOLUME_FLOOR = 0.5
PAD = 8

MESH = pl.DeviceIdType.MESH


def minmod(a, b):
    return jnp.maximum(jnp.minimum(a, b), 0.0) + jnp.minimum(jnp.maximum(a, b), 0.0)


def pressure_of(w, inverse):
    kinetic = w[1] * w[1] + w[2] * w[2] + w[3] * w[3]
    return GAMMA_LESS * (w[4] - 0.5 * kinetic * inverse)


def flux(w, d):
    inverse = 1.0 / w[0]
    u = w[d] * inverse
    p = pressure_of(w, inverse)
    out = [w[d], w[1] * u, w[2] * u, w[3] * u, (w[4] + p) * u]
    out[d] = out[d] + p
    return out


def face(left, right, d, half_open):
    fl, fr = flux(left, d), flux(right, d)
    return [
        ((fl[f] + fr[f]) + DISSIPATION * (left[f] - right[f])) * half_open for f in range(NF)
    ]


def kernel(
    state, volume, apertures, flags, out,
    buf1, buf2, ox, oy, oz, vol, flg, pk, rec_low, rec_high, gfix, sfix, afix, acc,
    first, scale, keep, gain, local_sem, send_sem, recv_sem, chain,
):
    _, X, Y, Z = state.shape
    F4 = 4 * X
    me = [lax.axis_index(a) for a in ("gx", "gy", "gz")]
    size = [lax.axis_size(a) for a in ("gx", "gy", "gz")]
    up = [{a: lax.rem(me[i] + 1, size[i])} for i, a in enumerate(("gx", "gy", "gz"))]
    down = [{a: lax.rem(me[i] + size[i] - 1, size[i])} for i, a in enumerate(("gx", "gy", "gz"))]

    rows = pl.ds(PAD, Y)
    loads = [
        (state, buf1.at[:, pl.ds(2, X), rows, :]),
        (apertures.at[0], ox.at[pl.ds(0, X)]),
        (apertures.at[1], oy.at[:, pl.ds(0, Y), :]),
        (apertures.at[2], oz),
        (volume, vol),
        (flags, flg),
    ]
    loads = [pltpu.make_async_copy(s, d, local_sem.at[i]) for i, (s, d) in enumerate(loads)]
    for load in loads:
        load.start()

    barrier = pltpu.get_barrier_semaphore()
    n_z = size[2]
    bottom, top = me[2] == 0, me[2] == n_z - 1
    for i in range(2):
        pl.semaphore_signal(barrier, inc=1, device_id=up[i], device_id_type=MESH)
        pl.semaphore_signal(barrier, inc=1, device_id=down[i], device_id_type=MESH)

    @pl.when(jnp.logical_not(top))
    def _():
        pl.semaphore_signal(barrier, inc=1, device_id=up[2], device_id_type=MESH)

    @pl.when(jnp.logical_not(bottom))
    def _():
        pl.semaphore_signal(barrier, inc=1, device_id=down[2], device_id_type=MESH)

    pl.semaphore_wait(barrier, 6 - jnp.where(top, 1, 0) - jnp.where(bottom, 1, 0))

    def remote(src, dst, slot, target):
        return pltpu.make_async_remote_copy(
            src_ref=src, dst_ref=dst, send_sem=send_sem.at[slot], recv_sem=recv_sem.at[slot],
            device_id=target, device_id_type=MESH,
        )

    def x_copies(src, x0, r, buf, slot):
        own = lambda lo: src.at[:, pl.ds(x0 + lo, 2), r, :]
        return (
            remote(own(0), buf.at[:, pl.ds(X + 2, 2), rows, :], slot, down[0]),
            remote(own(X - 2), buf.at[:, pl.ds(0, 2), rows, :], slot + 1, up[0]),
        )

    def y_copies(src, x0, y0, buf, slot):
        mid = pl.ds(x0, X)
        return (
            remote(src.at[:, mid, pl.ds(y0, 2), :],
                   buf.at[:, pl.ds(2, X), pl.ds(PAD + Y, 2), :], slot, down[1]),
            remote(src.at[:, mid, pl.ds(y0 + Y - 2, 2), :],
                   buf.at[:, pl.ds(2, X), pl.ds(PAD - 2, 2), :], slot + 1, up[1]),
        )

    def z_copies(stage, slot):
        return (
            remote(pk.at[stage], rec_high.at[stage], slot, down[2]),
            remote(pk.at[stage], rec_low.at[stage], slot + 1, up[2]),
        )

    xs1 = x_copies(state, 0, pl.ds(0, Y), buf1, 0)
    ys1 = y_copies(state, 0, 0, buf1, 2)
    ax = remote(apertures.at[0, pl.ds(0, 1)], ox.at[pl.ds(X, 1)], 4, down[0])
    ay = remote(apertures.at[1, :, pl.ds(0, 1), :], oy.at[:, pl.ds(Y, 1), :], 5, down[1])
    for c in xs1 + ys1 + (ax, ay):
        c.start()
    for load in loads:
        load.wait()

    lane = lax.broadcasted_iota(jnp.int32, (Y, Z), 1)
    quad = lax.rem(lane, 4)

    def pack(buf, stage):
        packed = jnp.zeros((Y, Z), jnp.float32)
        for f in range(NF + 1):
            for x in range(X):
                base = f * F4 + 4 * x
                value = buf[f, x + 2, PAD:PAD + Y, :] if f < NF else oz[x]
                inside = (lane >= base) & (lane < base + 4)
                packed = jnp.where(inside, pltpu.roll(value, base + 2, 1), packed)
        pk[stage] = packed

    pack(buf1, 0)
    zs1 = z_copies(0, 6)

    @pl.when(jnp.logical_not(bottom))
    def _():
        zs1[0].start()

    @pl.when(jnp.logical_not(top))
    def _():
        zs1[1].start()

    if n_z > 2:
        @pl.when(me[2] < n_z - 2)
        def _():
            pl.semaphore_wait(chain, 1)

        @pl.when((me[2] > 0) & (me[2] < n_z - 1))
        def _():
            pl.semaphore_signal(chain, inc=1, device_id=down[2], device_id_type=MESH)

    @pl.when(bottom)
    def _():
        zs1[0].start()

    limit = jnp.where(me[2] == 0, CUTZ, 0)
    for x in range(X):
        v = vol[x]
        fl = flg[x]
        weight = jnp.sum(jnp.where(lane < CUTZ, v, 0.0), axis=1, keepdims=True)
        excess = jnp.where((fl == 1) & (lane < limit), 1.0 - v, 0.0)
        scale[x] = jnp.where(fl != 2, 1.0 / jnp.maximum(v, VOLUME_FLOOR), 0.0)
        keep[x] = excess
        gain[x] = jnp.where(lane < limit, v / weight, 0.0)

    def boundary_z(stage):
        own = pk[stage]
        still = jnp.where(quad == 0, pltpu.roll(own, Z - 2, 1), pltpu.roll(own, Z - 1, 1))
        low = jnp.where(bottom, still, rec_low[stage])
        high = rec_high[0] if stage == 0 else jnp.where(top, rec_high[0], rec_high[stage])
        lefts, rights, slopes = [], [], []
        for c in (jnp.where(quad < 2, own, high), jnp.where(quad < 2, low, own)):
            d = c - pltpu.roll(c, 1, 1)
            s = minmod(d, pltpu.roll(d, Z - 1, 1))
            slopes.append(s)
            lefts.append(c + 0.5 * s)
            rights.append(c - 0.5 * s)
        first_lane = quad == 0
        left = jnp.where(first_lane, pltpu.roll(lefts[0], Z - 1, 1), lefts[1])
        right = jnp.where(
            first_lane, pltpu.roll(rights[0], Z - 2, 1), pltpu.roll(rights[1], Z - 1, 1)
        )
        sfix[...] = jnp.where(
            first_lane, pltpu.roll(slopes[0], Z - 1, 1), pltpu.roll(slopes[1], Z - 1, 1)
        )
        opening = jnp.where(
            first_lane, pltpu.roll(high, Z - 2, 1), pltpu.roll(own, Z - 1, 1)
        )
        ls = [pltpu.roll(left, Z - f * F4, 1) if f else left for f in range(NF)]
        rs = [pltpu.roll(right, Z - f * F4, 1) if f else right for f in range(NF)]
        opening = pltpu.roll(opening, Z - NF * F4, 1)
        live = lane < F4
        ls = [jnp.where(live & (quad < 2), w, 1.0) for w in ls]
        rs = [jnp.where(live & (quad < 2), w, 1.0) for w in rs]
        g = face(ls, rs, 3, 0.5 * opening)
        for f in range(NF):
            gfix[f] = g[f]
        afix[...] = opening

    def z_part(x, buf):
        v = [buf[f, x + 2, PAD:PAD + Y, :] for f in range(NF)]
        p = pressure_of(v, 1.0 / v[0])
        a = oz[x]
        shift = Z - (4 * x + 1)
        sl = []
        for f in range(NF):
            d = v[f] - pltpu.roll(v[f], 1, 1)
            s = minmod(d, pltpu.roll(d, Z - 1, 1))
            fix = pltpu.roll(sfix[...], lax.rem(2 * Z - (f * F4 + 4 * x + 1), Z), 1)
            sl.append(0.5 * jnp.where((lane == 0) | (lane == Z - 1), fix, s))
        left = [pltpu.roll(v[f] + sl[f], 1, 1) for f in range(NF)]
        right = [v[f] - sl[f] for f in range(NF)]
        g = face(left, right, 3, 0.5 * a)
        div = [acc[f, x] for f in range(NF)]
        for f in range(NF):
            fix = pltpu.roll(gfix[f], shift, 1)
            low = jnp.where(lane == 0, fix, g[f])
            high = jnp.where(lane == Z - 1, fix, pltpu.roll(g[f], Z - 1, 1))
            div[f] = div[f] + (high - low)
        a_high = jnp.where(
            lane == Z - 1, pltpu.roll(afix[...], shift, 1), pltpu.roll(a, Z - 1, 1)
        )
        div[3] = div[3] - p * (a_high - a)
        for f in range(NF):
            acc[f, x] = div[f]

    def y_part(x, buf):
        v = [buf[f, x + 2, PAD:PAD + Y, :] for f in range(NF)]
        p = pressure_of(v, 1.0 / v[0])
        E = Y + 8
        left, right, div = [], [], []
        for f in range(NF):
            c = buf[f, x + 2, PAD - 1:PAD - 1 + E, :]
            b = buf[f, x + 2, PAD - 2:PAD - 2 + E, :]
            n = buf[f, x + 2, PAD:PAD + E, :]
            s = 0.5 * minmod(c - b, n - c)
            left.append(c + s)
            right.append(pltpu.roll(c - s, E - 1, 0))
        a = oy[x]
        g = face(left, right, 2, 0.5 * a)
        for f in range(NF):
            div.append(pltpu.roll(g[f], E - 1, 0)[:Y] - g[f][:Y])
        div[2] = div[2] - p * (oy[x, 1:Y + 1, :] - oy[x, 0:Y, :])
        div[1] = div[1] - p * (ox[x + 1] - ox[x])
        for f in range(NF):
            acc[f, x] = div[f]

    def x_part(buf, finish):
        def load(f, x):
            return buf[f, x + 2, PAD:PAD + Y, :]

        def half_slope(x):
            return [
                0.5 * minmod(load(f, x) - load(f, x - 1), load(f, x + 1) - load(f, x))
                for f in range(NF)
            ]

        s = half_slope(-1)
        left = [load(f, -1) + s[f] for f in range(NF)]
        below = None
        for x in range(X + 1):
            s = half_slope(x)
            right = [load(f, x) - s[f] for f in range(NF)]
            g = face(left, right, 1, 0.5 * ox[x])
            left = [load(f, x) + s[f] for f in range(NF)]
            if x > 0:
                c = x - 1
                rates = []
                for f in range(NF):
                    base = -(acc[f, c] + (g[f] - below[f])) * scale[c]
                    moved = jnp.sum(keep[c] * base, axis=1, keepdims=True)
                    rates.append((1.0 - keep[c]) * base + gain[c] * moved)
                finish(c, rates)
            below = g

    def loop(part, buf):
        def body(x, carry):
            part(x, buf)
            return carry

        lax.fori_loop(0, X, body, 0)

    def arrive(copies):
        for c in copies:
            c.wait_recv()

    arrive(ys1 + (ax, ay))
    loop(y_part, buf1)
    zs1[0].wait_recv()

    @pl.when(jnp.logical_not(bottom))
    def _():
        zs1[1].wait_recv()

    boundary_z(0)
    loop(z_part, buf1)
    arrive(xs1)

    xs2 = x_copies(buf2, 2, rows, buf2, 8)
    ys2 = y_copies(buf2, 2, PAD, buf2, 10)
    zs2 = z_copies(1, 12)

    def finish_first(c, rates):
        for f in range(NF):
            first[f, c] = rates[f]
            buf2[f, c + 2, PAD:PAD + Y, :] = buf1[f, c + 2, PAD:PAD + Y, :] + TIME_STEP * rates[f]
        if c == 1:
            xs2[0].start()
        if c == X - 1:
            xs2[1].start()

    x_part(buf1, finish_first)
    for c in ys2:
        c.start()
    pack(buf2, 1)

    @pl.when(jnp.logical_not(bottom))
    def _():
        zs2[0].start()

    @pl.when(jnp.logical_not(top))
    def _():
        zs2[1].start()

    arrive(ys2)
    loop(y_part, buf2)

    @pl.when(jnp.logical_not(top))
    def _():
        zs2[0].wait_recv()

    @pl.when(jnp.logical_not(bottom))
    def _():
        zs2[1].wait_recv()

    boundary_z(1)
    loop(z_part, buf2)
    arrive(xs2)

    def finish_second(c, rates):
        for f in range(NF):
            out[f, c] = 0.5 * (first[f, c] + rates[f])

    x_part(buf2, finish_second)
    for c in xs1 + ys1 + (ax, ay, zs1[0]) + xs2 + ys2:
        c.wait_send()

    @pl.when(jnp.logical_not(top))
    def _():
        zs1[1].wait_send()
        zs2[1].wait_send()

    @pl.when(jnp.logical_not(bottom))
    def _():
        zs2[0].wait_send()


def on_device(state, volume, apertures, flags):
    _, X, Y, Z = state.shape
    f32 = jnp.float32
    wide = pltpu.VMEM((NF, X + 4, Y + 2 * PAD, Z), f32)
    cells = pltpu.VMEM((X, Y, Z), f32)
    fields = pltpu.VMEM((NF, X, Y, Z), f32)
    layer = pltpu.VMEM((Y, Z), f32)
    pair = pltpu.VMEM((2, Y, Z), f32)
    return pl.pallas_call(
        kernel,
        out_shape=jax.ShapeDtypeStruct(state.shape, f32),
        in_specs=[pl.BlockSpec(memory_space=pl.ANY)] * 4,
        out_specs=pl.BlockSpec(memory_space=pltpu.VMEM),
        scratch_shapes=[
            wide, wide,
            pltpu.VMEM((X + 1, Y, Z), f32),
            pltpu.VMEM((X, Y + 8, Z), f32),
            cells, cells, pltpu.VMEM((X, Y, Z), jnp.int32),
            pair, pair, pair,
            pltpu.VMEM((NF, Y, Z), f32), layer, layer,
            fields, fields, cells, cells, cells,
            pltpu.SemaphoreType.DMA((6,)),
            pltpu.SemaphoreType.DMA((14,)),
            pltpu.SemaphoreType.DMA((14,)),
            pltpu.SemaphoreType.REGULAR,
        ],
        compiler_params=pltpu.CompilerParams(collective_id=0, has_side_effects=True),
    )(state, volume, apertures, flags)


def solution(mesh):
    in_specs = (
        P(None, "gx", "gy", "gz"),
        P("gx", "gy", "gz"),
        P(None, "gx", "gy", "gz"),
        P("gx", "gy", "gz"),
    )
    return jax.shard_map(
        on_device, mesh=mesh, in_specs=in_specs, out_specs=P(None, "gx", "gy", "gz"),
        check_vma=False,
    )
```

```python
import jax
import jax.numpy as jnp
from jax import lax
from jax.experimental import pallas as pl
from jax.experimental.pallas import tpu as pltpu
from jax.sharding import PartitionSpec as P

CUTZ = 32
NF = 5
GAMMA_LESS = 0.4
DISSIPATION = 4.0
TIME_STEP = 0.02
VOLUME_FLOOR = 0.5
PAD = 8

MESH = pl.DeviceIdType.MESH


def minmod(a, b):
    return jnp.maximum(jnp.minimum(a, b), 0.0) + jnp.minimum(jnp.maximum(a, b), 0.0)


def pressure_of(w, inverse):
    kinetic = w[1] * w[1] + w[2] * w[2] + w[3] * w[3]
    return GAMMA_LESS * (w[4] - 0.5 * kinetic * inverse)


def flux(w, d):
    inverse = 1.0 / w[0]
    u = w[d] * inverse
    p = pressure_of(w, inverse)
    out = [w[d], w[1] * u, w[2] * u, w[3] * u, (w[4] + p) * u]
    out[d] = out[d] + p
    return out


def face(left, right, d, half_open):
    fl, fr = flux(left, d), flux(right, d)
    return [
        ((fl[f] + fr[f]) + DISSIPATION * (left[f] - right[f])) * half_open for f in range(NF)
    ]


def kernel(
    state, volume, apertures, flags, out,
    buf1, buf2, ox, oy, oz, vol, flg, pk, rec_low, rec_high, gfix, sfix, afix, acc,
    first, scale, keep, gain, local_sem, send_sem, recv_sem, chain, press,
):
    _, X, Y, Z = state.shape
    F4 = 4 * X
    me = [lax.axis_index(a) for a in ("gx", "gy", "gz")]
    size = [lax.axis_size(a) for a in ("gx", "gy", "gz")]
    up = [{a: lax.rem(me[i] + 1, size[i])} for i, a in enumerate(("gx", "gy", "gz"))]
    down = [{a: lax.rem(me[i] + size[i] - 1, size[i])} for i, a in enumerate(("gx", "gy", "gz"))]

    rows = pl.ds(PAD, Y)
    loads = [
        (state, buf1.at[:, pl.ds(2, X), rows, :]),
        (apertures.at[0], ox.at[pl.ds(0, X)]),
        (apertures.at[1], oy.at[:, pl.ds(0, Y), :]),
        (apertures.at[2], oz),
        (volume, vol),
        (flags, flg),
    ]
    loads = [pltpu.make_async_copy(s, d, local_sem.at[i]) for i, (s, d) in enumerate(loads)]
    for load in loads:
        load.start()

    barrier = pltpu.get_barrier_semaphore()
    n_z = size[2]
    bottom, top = me[2] == 0, me[2] == n_z - 1
    for i in range(2):
        pl.semaphore_signal(barrier, inc=1, device_id=up[i], device_id_type=MESH)
        pl.semaphore_signal(barrier, inc=1, device_id=down[i], device_id_type=MESH)

    @pl.when(jnp.logical_not(top))
    def _():
        pl.semaphore_signal(barrier, inc=1, device_id=up[2], device_id_type=MESH)

    @pl.when(jnp.logical_not(bottom))
    def _():
        pl.semaphore_signal(barrier, inc=1, device_id=down[2], device_id_type=MESH)

    pl.semaphore_wait(barrier, 6 - jnp.where(top, 1, 0) - jnp.where(bottom, 1, 0))

    def remote(src, dst, slot, target):
        return pltpu.make_async_remote_copy(
            src_ref=src, dst_ref=dst, send_sem=send_sem.at[slot], recv_sem=recv_sem.at[slot],
            device_id=target, device_id_type=MESH,
        )

    def x_copies(src, x0, r, buf, slot):
        own = lambda lo: src.at[:, pl.ds(x0 + lo, 2), r, :]
        return (
            remote(own(0), buf.at[:, pl.ds(X + 2, 2), rows, :], slot, down[0]),
            remote(own(X - 2), buf.at[:, pl.ds(0, 2), rows, :], slot + 1, up[0]),
        )

    def y_copies(src, x0, y0, buf, slot):
        mid = pl.ds(x0, X)
        return (
            remote(src.at[:, mid, pl.ds(y0, 2), :],
                   buf.at[:, pl.ds(2, X), pl.ds(PAD + Y, 2), :], slot, down[1]),
            remote(src.at[:, mid, pl.ds(y0 + Y - 2, 2), :],
                   buf.at[:, pl.ds(2, X), pl.ds(PAD - 2, 2), :], slot + 1, up[1]),
        )

    def z_copies(stage, slot):
        return (
            remote(pk.at[stage], rec_high.at[stage], slot, down[2]),
            remote(pk.at[stage], rec_low.at[stage], slot + 1, up[2]),
        )

    xs1 = x_copies(state, 0, pl.ds(0, Y), buf1, 0)
    ys1 = y_copies(state, 0, 0, buf1, 2)
    ax = remote(apertures.at[0, pl.ds(0, 1)], ox.at[pl.ds(X, 1)], 4, down[0])
    ay = remote(apertures.at[1, :, pl.ds(0, 1), :], oy.at[:, pl.ds(Y, 1), :], 5, down[1])
    for c in (ax,) + xs1 + (ay,) + ys1:
        c.start()
    for load in loads:
        load.wait()

    lane = lax.broadcasted_iota(jnp.int32, (Y, Z), 1)
    quad = lax.rem(lane, 4)

    def pack(buf, stage):
        packed = jnp.zeros((Y, Z), jnp.float32)
        for f in range(NF + 1):
            for x in range(X):
                base = f * F4 + 4 * x
                value = buf[f, x + 2, PAD:PAD + Y, :] if f < NF else oz[x]
                inside = (lane >= base) & (lane < base + 4)
                packed = jnp.where(inside, pltpu.roll(value, base + 2, 1), packed)
        pk[stage] = packed

    pack(buf1, 0)
    zs1 = z_copies(0, 6)

    @pl.when(jnp.logical_not(bottom))
    def _():
        zs1[0].start()

    @pl.when(jnp.logical_not(top))
    def _():
        zs1[1].start()

    if n_z > 2:
        @pl.when(me[2] < n_z - 2)
        def _():
            pl.semaphore_wait(chain, 1)

        @pl.when((me[2] > 0) & (me[2] < n_z - 1))
        def _():
            pl.semaphore_signal(chain, inc=1, device_id=down[2], device_id_type=MESH)

    @pl.when(bottom)
    def _():
        zs1[0].start()

    limit = jnp.where(me[2] == 0, CUTZ, 0)
    for x in range(X):
        v = vol[x]
        fl = flg[x]
        weight = jnp.sum(jnp.where(lane < CUTZ, v, 0.0), axis=1, keepdims=True)
        excess = jnp.where((fl == 1) & (lane < limit), 1.0 - v, 0.0)
        scale[x] = jnp.where(fl != 2, 1.0 / jnp.maximum(v, VOLUME_FLOOR), 0.0)
        keep[x] = excess
        gain[x] = jnp.where(lane < limit, v / weight, 0.0)

    def boundary_z(stage):
        own = pk[stage]
        still = jnp.where(quad == 0, pltpu.roll(own, Z - 2, 1), pltpu.roll(own, Z - 1, 1))
        low = jnp.where(bottom, still, rec_low[stage])
        high = rec_high[0] if stage == 0 else jnp.where(top, rec_high[0], rec_high[stage])
        lefts, rights, slopes = [], [], []
        for c in (jnp.where(quad < 2, own, high), jnp.where(quad < 2, low, own)):
            d = c - pltpu.roll(c, 1, 1)
            s = minmod(d, pltpu.roll(d, Z - 1, 1))
            slopes.append(s)
            lefts.append(c + 0.5 * s)
            rights.append(c - 0.5 * s)
        first_lane = quad == 0
        left = jnp.where(first_lane, pltpu.roll(lefts[0], Z - 1, 1), lefts[1])
        right = jnp.where(
            first_lane, pltpu.roll(rights[0], Z - 2, 1), pltpu.roll(rights[1], Z - 1, 1)
        )
        sfix[...] = jnp.where(
            first_lane, pltpu.roll(slopes[0], Z - 1, 1), pltpu.roll(slopes[1], Z - 1, 1)
        )
        opening = jnp.where(
            first_lane, pltpu.roll(high, Z - 2, 1), pltpu.roll(own, Z - 1, 1)
        )
        ls = [pltpu.roll(left, Z - f * F4, 1) if f else left for f in range(NF)]
        rs = [pltpu.roll(right, Z - f * F4, 1) if f else right for f in range(NF)]
        opening = pltpu.roll(opening, Z - NF * F4, 1)
        live = lane < F4
        ls = [jnp.where(live & (quad < 2), w, 1.0) for w in ls]
        rs = [jnp.where(live & (quad < 2), w, 1.0) for w in rs]
        g = face(ls, rs, 3, 0.5 * opening)
        for f in range(NF):
            gfix[f] = g[f]
        afix[...] = opening

    def z_part(x, buf):
        v = [buf[f, x + 2, PAD:PAD + Y, :] for f in range(NF)]
        p = press[x]
        a = oz[x]
        shift = Z - (4 * x + 1)
        sl = []
        for f in range(NF):
            d = v[f] - pltpu.roll(v[f], 1, 1)
            s = minmod(d, pltpu.roll(d, Z - 1, 1))
            fix = pltpu.roll(sfix[...], lax.rem(2 * Z - (f * F4 + 4 * x + 1), Z), 1)
            sl.append(0.5 * jnp.where((lane == 0) | (lane == Z - 1), fix, s))
        left = [pltpu.roll(v[f] + sl[f], 1, 1) for f in range(NF)]
        right = [v[f] - sl[f] for f in range(NF)]
        g = face(left, right, 3, 0.5 * a)
        div = [acc[f, x] for f in range(NF)]
        for f in range(NF):
            fix = pltpu.roll(gfix[f], shift, 1)
            low = jnp.where(lane == 0, fix, g[f])
            high = jnp.where(lane == Z - 1, fix, pltpu.roll(g[f], Z - 1, 1))
            div[f] = div[f] + (high - low)
        a_high = jnp.where(
            lane == Z - 1, pltpu.roll(afix[...], shift, 1), pltpu.roll(a, Z - 1, 1)
        )
        div[3] = div[3] - p * (a_high - a)
        for f in range(NF):
            acc[f, x] = div[f]

    def y_part(x, buf):
        v = [buf[f, x + 2, PAD:PAD + Y, :] for f in range(NF)]
        p = pressure_of(v, 1.0 / v[0])
        E = Y + 8
        left, right, div = [], [], []
        for f in range(NF):
            c = buf[f, x + 2, PAD - 1:PAD - 1 + E, :]
            b = buf[f, x + 2, PAD - 2:PAD - 2 + E, :]
            n = buf[f, x + 2, PAD:PAD + E, :]
            s = 0.5 * minmod(c - b, n - c)
            left.append(c + s)
            right.append(pltpu.roll(c - s, E - 1, 0))
        a = oy[x]
        g = face(left, right, 2, 0.5 * a)
        for f in range(NF):
            div.append(pltpu.roll(g[f], E - 1, 0)[:Y] - g[f][:Y])
        div[2] = div[2] - p * (oy[x, 1:Y + 1, :] - oy[x, 0:Y, :])
        press[x] = p
        for f in range(NF):
            acc[f, x] = div[f]

    def x_part(buf, finish):
        def load(f, x):
            return buf[f, x + 2, PAD:PAD + Y, :]

        def half_slope(x):
            return [
                0.5 * minmod(load(f, x) - load(f, x - 1), load(f, x + 1) - load(f, x))
                for f in range(NF)
            ]

        s = half_slope(-1)
        left = [load(f, -1) + s[f] for f in range(NF)]
        below = None
        for x in range(X + 1):
            s = half_slope(x)
            right = [load(f, x) - s[f] for f in range(NF)]
            g = face(left, right, 1, 0.5 * ox[x])
            left = [load(f, x) + s[f] for f in range(NF)]
            if x > 0:
                c = x - 1
                rates = []
                for f in range(NF):
                    total = acc[f, c] + (g[f] - below[f])
                    if f == 1:
                        total = total - press[c] * (ox[x] - ox[c])
                    base = -total * scale[c]
                    moved = jnp.sum(keep[c] * base, axis=1, keepdims=True)
                    rates.append((1.0 - keep[c]) * base + gain[c] * moved)
                finish(c, rates)
            below = g

    def loop(part, buf):
        def body(x, carry):
            part(x, buf)
            return carry

        lax.fori_loop(0, X, body, 0)

    def arrive(copies):
        for c in copies:
            c.wait_recv()

    arrive(ys1 + (ay,))
    loop(y_part, buf1)
    zs1[0].wait_recv()

    @pl.when(jnp.logical_not(bottom))
    def _():
        zs1[1].wait_recv()

    boundary_z(0)
    loop(z_part, buf1)
    arrive((ax,) + xs1)

    xs2 = x_copies(buf2, 2, rows, buf2, 8)
    ys2 = y_copies(buf2, 2, PAD, buf2, 10)
    zs2 = z_copies(1, 12)

    def finish_first(c, rates):
        for f in range(NF):
            first[f, c] = rates[f]
            buf2[f, c + 2, PAD:PAD + Y, :] = buf1[f, c + 2, PAD:PAD + Y, :] + TIME_STEP * rates[f]
        if c == 1:
            xs2[0].start()
        if c == X - 1:
            xs2[1].start()

    x_part(buf1, finish_first)
    for c in ys2:
        c.start()
    pack(buf2, 1)

    @pl.when(jnp.logical_not(bottom))
    def _():
        zs2[0].start()

    @pl.when(jnp.logical_not(top))
    def _():
        zs2[1].start()

    arrive(ys2)
    loop(y_part, buf2)

    @pl.when(jnp.logical_not(top))
    def _():
        zs2[0].wait_recv()

    @pl.when(jnp.logical_not(bottom))
    def _():
        zs2[1].wait_recv()

    boundary_z(1)
    loop(z_part, buf2)
    arrive(xs2)

    def finish_second(c, rates):
        for f in range(NF):
            out[f, c] = 0.5 * (first[f, c] + rates[f])

    x_part(buf2, finish_second)
    for c in xs1 + ys1 + (ax, ay, zs1[0]) + xs2 + ys2:
        c.wait_send()

    @pl.when(jnp.logical_not(top))
    def _():
        zs1[1].wait_send()
        zs2[1].wait_send()

    @pl.when(jnp.logical_not(bottom))
    def _():
        zs2[0].wait_send()


def on_device(state, volume, apertures, flags):
    _, X, Y, Z = state.shape
    f32 = jnp.float32
    wide = pltpu.VMEM((NF, X + 4, Y + 2 * PAD, Z), f32)
    cells = pltpu.VMEM((X, Y, Z), f32)
    fields = pltpu.VMEM((NF, X, Y, Z), f32)
    layer = pltpu.VMEM((Y, Z), f32)
    pair = pltpu.VMEM((2, Y, Z), f32)
    return pl.pallas_call(
        kernel,
        out_shape=pltpu.VMEM(state.shape, f32),
        in_specs=[pl.BlockSpec(memory_space=pl.ANY)] * 4,
        out_specs=pl.BlockSpec(memory_space=pltpu.VMEM),
        scratch_shapes=[
            wide, wide,
            pltpu.VMEM((X + 1, Y, Z), f32),
            pltpu.VMEM((X, Y + 8, Z), f32),
            cells, cells, pltpu.VMEM((X, Y, Z), jnp.int32),
            pair, pair, pair,
            pltpu.VMEM((NF, Y, Z), f32), layer, layer,
            fields, fields, cells, cells, cells,
            pltpu.SemaphoreType.DMA((6,)),
            pltpu.SemaphoreType.DMA((14,)),
            pltpu.SemaphoreType.DMA((14,)),
            pltpu.SemaphoreType.REGULAR,
            cells,
        ],
        compiler_params=pltpu.CompilerParams(collective_id=0, has_side_effects=True),
    )(state, volume, apertures, flags)


def solution(mesh):
    in_specs = (
        P(None, "gx", "gy", "gz"),
        P("gx", "gy", "gz"),
        P(None, "gx", "gy", "gz"),
        P("gx", "gy", "gz"),
    )
    return jax.shard_map(
        on_device, mesh=mesh, in_specs=in_specs, out_specs=P(None, "gx", "gy", "gz"),
        check_vma=False,
    )
```

```python
import jax
import jax.numpy as jnp
from jax import lax
from jax.experimental import pallas as pl
from jax.experimental.pallas import tpu as pltpu
from jax.sharding import PartitionSpec as P

CUTZ = 32
NF = 5
GAMMA_LESS = 0.4
DISSIPATION = 4.0
TIME_STEP = 0.02
VOLUME_FLOOR = 0.5
PAD = 8

MESH = pl.DeviceIdType.MESH


def minmod(a, b):
    return jnp.maximum(jnp.minimum(a, b), 0.0) + jnp.minimum(jnp.maximum(a, b), 0.0)


def pressure_of(w, inverse):
    kinetic = w[1] * w[1] + w[2] * w[2] + w[3] * w[3]
    return GAMMA_LESS * (w[4] - 0.5 * kinetic * inverse)


def flux(w, d):
    inverse = 1.0 / w[0]
    u = w[d] * inverse
    p = pressure_of(w, inverse)
    out = [w[d], w[1] * u, w[2] * u, w[3] * u, (w[4] + p) * u]
    out[d] = out[d] + p
    return out


def face(left, right, d, half_open):
    fl, fr = flux(left, d), flux(right, d)
    return [
        ((fl[f] + fr[f]) + DISSIPATION * (left[f] - right[f])) * half_open for f in range(NF)
    ]


def kernel(
    state, volume, apertures, flags, out,
    buf1, buf2, ox, oy, oz, vol, flg, pk, rec_low, rec_high, gfix, sfix, afix, acc,
    first, scale, keep, gain, local_sem, send_sem, recv_sem, chain, press,
):
    _, X, Y, Z = state.shape
    F4 = 4 * X
    me = [lax.axis_index(a) for a in ("gx", "gy", "gz")]
    size = [lax.axis_size(a) for a in ("gx", "gy", "gz")]
    up = [{a: lax.rem(me[i] + 1, size[i])} for i, a in enumerate(("gx", "gy", "gz"))]
    down = [{a: lax.rem(me[i] + size[i] - 1, size[i])} for i, a in enumerate(("gx", "gy", "gz"))]

    rows = pl.ds(PAD, Y)
    loads = [
        (state, buf1.at[:, pl.ds(2, X), rows, :]),
        (apertures.at[0], ox.at[pl.ds(0, X)]),
        (apertures.at[1], oy.at[:, pl.ds(0, Y), :]),
        (apertures.at[2], oz),
        (volume, vol),
        (flags, flg),
    ]
    loads = [pltpu.make_async_copy(s, d, local_sem.at[i]) for i, (s, d) in enumerate(loads)]
    for load in loads:
        load.start()

    barrier = pltpu.get_barrier_semaphore()
    n_z = size[2]
    bottom, top = me[2] == 0, me[2] == n_z - 1
    for i in range(2):
        pl.semaphore_signal(barrier, inc=1, device_id=up[i], device_id_type=MESH)
        pl.semaphore_signal(barrier, inc=1, device_id=down[i], device_id_type=MESH)

    @pl.when(jnp.logical_not(top))
    def _():
        pl.semaphore_signal(barrier, inc=1, device_id=up[2], device_id_type=MESH)

    @pl.when(jnp.logical_not(bottom))
    def _():
        pl.semaphore_signal(barrier, inc=1, device_id=down[2], device_id_type=MESH)

    pl.semaphore_wait(barrier, 6 - jnp.where(top, 1, 0) - jnp.where(bottom, 1, 0))

    def remote(src, dst, slot, target):
        return pltpu.make_async_remote_copy(
            src_ref=src, dst_ref=dst, send_sem=send_sem.at[slot], recv_sem=recv_sem.at[slot],
            device_id=target, device_id_type=MESH,
        )

    def x_copies(src, x0, r, buf, slot):
        own = lambda lo: src.at[:, pl.ds(x0 + lo, 2), r, :]
        return (
            remote(own(0), buf.at[:, pl.ds(X + 2, 2), rows, :], slot, down[0]),
            remote(own(X - 2), buf.at[:, pl.ds(0, 2), rows, :], slot + 1, up[0]),
        )

    def y_copies(src, x0, y0, buf, slot):
        mid = pl.ds(x0, X)
        return (
            remote(src.at[:, mid, pl.ds(y0, 2), :],
                   buf.at[:, pl.ds(2, X), pl.ds(PAD + Y, 2), :], slot, down[1]),
            remote(src.at[:, mid, pl.ds(y0 + Y - 2, 2), :],
                   buf.at[:, pl.ds(2, X), pl.ds(PAD - 2, 2), :], slot + 1, up[1]),
        )

    def z_copies(stage, slot):
        return (
            remote(pk.at[stage], rec_high.at[stage], slot, down[2]),
            remote(pk.at[stage], rec_low.at[stage], slot + 1, up[2]),
        )

    xs1 = x_copies(state, 0, pl.ds(0, Y), buf1, 0)
    ys1 = y_copies(state, 0, 0, buf1, 2)
    ax = remote(apertures.at[0, pl.ds(0, 1)], ox.at[pl.ds(X, 1)], 4, down[0])
    ay = remote(apertures.at[1, :, pl.ds(0, 1), :], oy.at[:, pl.ds(Y, 1), :], 5, down[1])
    for c in (ax,) + xs1 + (ay,) + ys1:
        c.start()
    for load in loads:
        load.wait()

    lane = lax.broadcasted_iota(jnp.int32, (Y, Z), 1)
    quad = lax.rem(lane, 4)

    def pack(buf, stage):
        packed = jnp.zeros((Y, Z), jnp.float32)
        for f in range(NF + 1):
            for x in range(X):
                base = f * F4 + 4 * x
                value = buf[f, x + 2, PAD:PAD + Y, :] if f < NF else oz[x]
                inside = (lane >= base) & (lane < base + 4)
                packed = jnp.where(inside, pltpu.roll(value, base + 2, 1), packed)
        pk[stage] = packed

    pack(buf1, 0)
    zs1 = z_copies(0, 6)

    @pl.when(jnp.logical_not(bottom))
    def _():
        zs1[0].start()

    @pl.when(jnp.logical_not(top))
    def _():
        zs1[1].start()

    if n_z > 2:
        @pl.when(me[2] < n_z - 2)
        def _():
            pl.semaphore_wait(chain, 1)

        @pl.when((me[2] > 0) & (me[2] < n_z - 1))
        def _():
            pl.semaphore_signal(chain, inc=1, device_id=down[2], device_id_type=MESH)

    @pl.when(bottom)
    def _():
        zs1[0].start()

    limit = jnp.where(me[2] == 0, CUTZ, 0)
    for x in range(X):
        v = vol[x]
        fl = flg[x]
        weight = jnp.sum(jnp.where(lane < CUTZ, v, 0.0), axis=1, keepdims=True)
        excess = jnp.where((fl == 1) & (lane < limit), 1.0 - v, 0.0)
        scale[x] = jnp.where(fl != 2, 1.0 / jnp.maximum(v, VOLUME_FLOOR), 0.0)
        keep[x] = excess
        gain[x] = jnp.where(lane < limit, v / weight, 0.0)

    def boundary_z(stage):
        own = pk[stage]
        still = jnp.where(quad == 0, pltpu.roll(own, Z - 2, 1), pltpu.roll(own, Z - 1, 1))
        low = jnp.where(bottom, still, rec_low[stage])
        high = rec_high[0] if stage == 0 else jnp.where(top, rec_high[0], rec_high[stage])
        lefts, rights, slopes = [], [], []
        for c in (jnp.where(quad < 2, own, high), jnp.where(quad < 2, low, own)):
            d = c - pltpu.roll(c, 1, 1)
            s = minmod(d, pltpu.roll(d, Z - 1, 1))
            slopes.append(s)
            lefts.append(c + 0.5 * s)
            rights.append(c - 0.5 * s)
        first_lane = quad == 0
        left = jnp.where(first_lane, pltpu.roll(lefts[0], Z - 1, 1), lefts[1])
        right = jnp.where(
            first_lane, pltpu.roll(rights[0], Z - 2, 1), pltpu.roll(rights[1], Z - 1, 1)
        )
        sfix[...] = jnp.where(
            first_lane, pltpu.roll(slopes[0], Z - 1, 1), pltpu.roll(slopes[1], Z - 1, 1)
        )
        opening = jnp.where(
            first_lane, pltpu.roll(high, Z - 2, 1), pltpu.roll(own, Z - 1, 1)
        )
        ls = [pltpu.roll(left, Z - f * F4, 1) if f else left for f in range(NF)]
        rs = [pltpu.roll(right, Z - f * F4, 1) if f else right for f in range(NF)]
        opening = pltpu.roll(opening, Z - NF * F4, 1)
        live = lane < F4
        ls = [jnp.where(live & (quad < 2), w, 1.0) for w in ls]
        rs = [jnp.where(live & (quad < 2), w, 1.0) for w in rs]
        g = face(ls, rs, 3, 0.5 * opening)
        for f in range(NF):
            gfix[f] = g[f]
        afix[...] = opening

    def z_part(x, buf):
        v = [buf[f, x + 2, PAD:PAD + Y, :] for f in range(NF)]
        p = press[x]
        a = oz[x]
        shift = Z - (4 * x + 1)
        sl = []
        for f in range(NF):
            d = v[f] - pltpu.roll(v[f], 1, 1)
            s = minmod(d, pltpu.roll(d, Z - 1, 1))
            fix = pltpu.roll(sfix[...], lax.rem(2 * Z - (f * F4 + 4 * x + 1), Z), 1)
            sl.append(0.5 * jnp.where((lane == 0) | (lane == Z - 1), fix, s))
        left = [pltpu.roll(v[f] + sl[f], 1, 1) for f in range(NF)]
        right = [v[f] - sl[f] for f in range(NF)]
        g = face(left, right, 3, 0.5 * a)
        div = [acc[f, x] for f in range(NF)]
        for f in range(NF):
            fix = pltpu.roll(gfix[f], shift, 1)
            low = jnp.where(lane == 0, fix, g[f])
            high = jnp.where(lane == Z - 1, fix, pltpu.roll(g[f], Z - 1, 1))
            div[f] = div[f] + (high - low)
        a_high = jnp.where(
            lane == Z - 1, pltpu.roll(afix[...], shift, 1), pltpu.roll(a, Z - 1, 1)
        )
        div[3] = div[3] - p * (a_high - a)
        for f in range(NF):
            acc[f, x] = div[f]

    def y_part(x, buf):
        v = [buf[f, x + 2, PAD:PAD + Y, :] for f in range(NF)]
        p = pressure_of(v, 1.0 / v[0])
        E = Y + 8
        left, right, div = [], [], []
        for f in range(NF):
            c = buf[f, x + 2, PAD - 1:PAD - 1 + E, :]
            b = buf[f, x + 2, PAD - 2:PAD - 2 + E, :]
            n = buf[f, x + 2, PAD:PAD + E, :]
            s = 0.5 * minmod(c - b, n - c)
            left.append(c + s)
            right.append(pltpu.roll(c - s, E - 1, 0))
        a = oy[x]
        g = face(left, right, 2, 0.5 * a)
        for f in range(NF):
            div.append(pltpu.roll(g[f], E - 1, 0)[:Y] - g[f][:Y])
        div[2] = div[2] - p * (oy[x, 1:Y + 1, :] - oy[x, 0:Y, :])
        press[x] = p
        for f in range(NF):
            acc[f, x] = div[f]

    def x_part(buf, finish):
        def load(f, x):
            return buf[f, x + 2, PAD:PAD + Y, :]

        def half_slope(x):
            return [
                0.5 * minmod(load(f, x) - load(f, x - 1), load(f, x + 1) - load(f, x))
                for f in range(NF)
            ]

        s = half_slope(-1)
        left = [load(f, -1) + s[f] for f in range(NF)]
        below = None
        for x in range(X + 1):
            s = half_slope(x)
            right = [load(f, x) - s[f] for f in range(NF)]
            g = face(left, right, 1, 0.5 * ox[x])
            left = [load(f, x) + s[f] for f in range(NF)]
            if x > 0:
                c = x - 1
                rates = []
                for f in range(NF):
                    total = acc[f, c] + (g[f] - below[f])
                    if f == 1:
                        total = total - press[c] * (ox[x] - ox[c])
                    base = -total * scale[c]
                    moved = jnp.sum(keep[c] * base, axis=1, keepdims=True)
                    rates.append((1.0 - keep[c]) * base + gain[c] * moved)
                finish(c, rates)
            below = g

    def loop(part, buf):
        def body(x, carry):
            part(x, buf)
            return carry

        lax.fori_loop(0, X, body, 0, unroll=True)

    def arrive(copies):
        for c in copies:
            c.wait_recv()

    arrive(ys1 + (ay,))
    loop(y_part, buf1)
    zs1[0].wait_recv()

    @pl.when(jnp.logical_not(bottom))
    def _():
        zs1[1].wait_recv()

    boundary_z(0)
    loop(z_part, buf1)
    arrive((ax,) + xs1)

    xs2 = x_copies(buf2, 2, rows, buf2, 8)
    ys2 = y_copies(buf2, 2, PAD, buf2, 10)
    zs2 = z_copies(1, 12)

    def finish_first(c, rates):
        for f in range(NF):
            first[f, c] = rates[f]
            buf2[f, c + 2, PAD:PAD + Y, :] = buf1[f, c + 2, PAD:PAD + Y, :] + TIME_STEP * rates[f]
        if c == 1:
            xs2[0].start()
        if c == X - 1:
            xs2[1].start()

    x_part(buf1, finish_first)
    for c in ys2:
        c.start()
    pack(buf2, 1)

    @pl.when(jnp.logical_not(bottom))
    def _():
        zs2[0].start()

    @pl.when(jnp.logical_not(top))
    def _():
        zs2[1].start()

    arrive(ys2)
    loop(y_part, buf2)

    @pl.when(jnp.logical_not(top))
    def _():
        zs2[0].wait_recv()

    @pl.when(jnp.logical_not(bottom))
    def _():
        zs2[1].wait_recv()

    boundary_z(1)
    loop(z_part, buf2)
    arrive(xs2)

    def finish_second(c, rates):
        for f in range(NF):
            out[f, c] = 0.5 * (first[f, c] + rates[f])

    x_part(buf2, finish_second)
    for c in xs1 + ys1 + (ax, ay, zs1[0]) + xs2 + ys2:
        c.wait_send()

    @pl.when(jnp.logical_not(top))
    def _():
        zs1[1].wait_send()
        zs2[1].wait_send()

    @pl.when(jnp.logical_not(bottom))
    def _():
        zs2[0].wait_send()


def on_device(state, volume, apertures, flags):
    _, X, Y, Z = state.shape
    f32 = jnp.float32
    wide = pltpu.VMEM((NF, X + 4, Y + 2 * PAD, Z), f32)
    cells = pltpu.VMEM((X, Y, Z), f32)
    fields = pltpu.VMEM((NF, X, Y, Z), f32)
    layer = pltpu.VMEM((Y, Z), f32)
    pair = pltpu.VMEM((2, Y, Z), f32)
    return pl.pallas_call(
        kernel,
        out_shape=pltpu.VMEM(state.shape, f32),
        in_specs=[pl.BlockSpec(memory_space=pl.ANY)] * 4,
        out_specs=pl.BlockSpec(memory_space=pltpu.VMEM),
        scratch_shapes=[
            wide, wide,
            pltpu.VMEM((X + 1, Y, Z), f32),
            pltpu.VMEM((X, Y + 8, Z), f32),
            cells, cells, pltpu.VMEM((X, Y, Z), jnp.int32),
            pair, pair, pair,
            pltpu.VMEM((NF, Y, Z), f32), layer, layer,
            fields, fields, cells, cells, cells,
            pltpu.SemaphoreType.DMA((6,)),
            pltpu.SemaphoreType.DMA((14,)),
            pltpu.SemaphoreType.DMA((14,)),
            pltpu.SemaphoreType.REGULAR,
            cells,
        ],
        compiler_params=pltpu.CompilerParams(collective_id=0, has_side_effects=True),
    )(state, volume, apertures, flags)


def solution(mesh):
    in_specs = (
        P(None, "gx", "gy", "gz"),
        P("gx", "gy", "gz"),
        P(None, "gx", "gy", "gz"),
        P("gx", "gy", "gz"),
    )
    return jax.shard_map(
        on_device, mesh=mesh, in_specs=in_specs, out_specs=P(None, "gx", "gy", "gz"),
        check_vma=False,
    )
```

```python
import jax
import jax.numpy as jnp
from jax import lax
from jax.experimental import pallas as pl
from jax.experimental.pallas import tpu as pltpu
from jax.sharding import PartitionSpec as P

CUTZ = 32
NF = 5
GAMMA_LESS = 0.4
DISSIPATION = 4.0
TIME_STEP = 0.02
VOLUME_FLOOR = 0.5
PAD = 8

MESH = pl.DeviceIdType.MESH


def minmod(a, b):
    return jnp.maximum(jnp.minimum(a, b), 0.0) + jnp.minimum(jnp.maximum(a, b), 0.0)


def pressure_of(w, inverse):
    kinetic = w[1] * w[1] + w[2] * w[2] + w[3] * w[3]
    return GAMMA_LESS * (w[4] - 0.5 * kinetic * inverse)


def flux(w, d):
    inverse = 1.0 / w[0]
    u = w[d] * inverse
    p = pressure_of(w, inverse)
    out = [w[d], w[1] * u, w[2] * u, w[3] * u, (w[4] + p) * u]
    out[d] = out[d] + p
    return out


def face(left, right, d, half_open):
    fl, fr = flux(left, d), flux(right, d)
    return [
        ((fl[f] + fr[f]) + DISSIPATION * (left[f] - right[f])) * half_open for f in range(NF)
    ]


def kernel(
    state, volume, apertures, flags, out,
    buf1, buf2, ox, oy, oz, vol, flg, pk, rec_low, rec_high, gfix, sfix, afix, acc,
    first, scale, keep, gain, local_sem, send_sem, recv_sem, chain, press, inner,
):
    _, X, Y, Z = state.shape
    F4 = 4 * X
    me = [lax.axis_index(a) for a in ("gx", "gy", "gz")]
    size = [lax.axis_size(a) for a in ("gx", "gy", "gz")]
    up = [{a: lax.rem(me[i] + 1, size[i])} for i, a in enumerate(("gx", "gy", "gz"))]
    down = [{a: lax.rem(me[i] + size[i] - 1, size[i])} for i, a in enumerate(("gx", "gy", "gz"))]

    rows = pl.ds(PAD, Y)
    loads = [
        (state, buf1.at[:, pl.ds(2, X), rows, :]),
        (apertures.at[0], ox.at[pl.ds(0, X)]),
        (apertures.at[1], oy.at[:, pl.ds(0, Y), :]),
        (apertures.at[2], oz),
        (volume, vol),
        (flags, flg),
    ]
    loads = [pltpu.make_async_copy(s, d, local_sem.at[i]) for i, (s, d) in enumerate(loads)]
    for load in loads:
        load.start()

    barrier = pltpu.get_barrier_semaphore()
    n_z = size[2]
    bottom, top = me[2] == 0, me[2] == n_z - 1
    for i in range(2):
        pl.semaphore_signal(barrier, inc=1, device_id=up[i], device_id_type=MESH)
        pl.semaphore_signal(barrier, inc=1, device_id=down[i], device_id_type=MESH)

    @pl.when(jnp.logical_not(top))
    def _():
        pl.semaphore_signal(barrier, inc=1, device_id=up[2], device_id_type=MESH)

    @pl.when(jnp.logical_not(bottom))
    def _():
        pl.semaphore_signal(barrier, inc=1, device_id=down[2], device_id_type=MESH)

    pl.semaphore_wait(barrier, 6 - jnp.where(top, 1, 0) - jnp.where(bottom, 1, 0))

    def remote(src, dst, slot, target):
        return pltpu.make_async_remote_copy(
            src_ref=src, dst_ref=dst, send_sem=send_sem.at[slot], recv_sem=recv_sem.at[slot],
            device_id=target, device_id_type=MESH,
        )

    def x_copies(src, x0, r, buf, slot):
        own = lambda lo: src.at[:, pl.ds(x0 + lo, 2), r, :]
        return (
            remote(own(0), buf.at[:, pl.ds(X + 2, 2), rows, :], slot, down[0]),
            remote(own(X - 2), buf.at[:, pl.ds(0, 2), rows, :], slot + 1, up[0]),
        )

    def y_copies(src, x0, y0, buf, slot):
        mid = pl.ds(x0, X)
        return (
            remote(src.at[:, mid, pl.ds(y0, 2), :],
                   buf.at[:, pl.ds(2, X), pl.ds(PAD + Y, 2), :], slot, down[1]),
            remote(src.at[:, mid, pl.ds(y0 + Y - 2, 2), :],
                   buf.at[:, pl.ds(2, X), pl.ds(PAD - 2, 2), :], slot + 1, up[1]),
        )

    def z_copies(stage, slot):
        return (
            remote(pk.at[stage], rec_high.at[stage], slot, down[2]),
            remote(pk.at[stage], rec_low.at[stage], slot + 1, up[2]),
        )

    xs1 = x_copies(state, 0, pl.ds(0, Y), buf1, 0)
    ys1 = y_copies(state, 0, 0, buf1, 2)
    ax = remote(apertures.at[0, pl.ds(0, 1)], ox.at[pl.ds(X, 1)], 4, down[0])
    ay = remote(apertures.at[1, :, pl.ds(0, 1), :], oy.at[:, pl.ds(Y, 1), :], 5, down[1])
    for c in (ax,) + xs1 + (ay,) + ys1:
        c.start()
    for load in loads:
        load.wait()

    lane = lax.broadcasted_iota(jnp.int32, (Y, Z), 1)
    quad = lax.rem(lane, 4)

    def pack(buf, stage):
        packed = jnp.zeros((Y, Z), jnp.float32)
        for f in range(NF + 1):
            for x in range(X):
                base = f * F4 + 4 * x
                value = buf[f, x + 2, PAD:PAD + Y, :] if f < NF else oz[x]
                inside = (lane >= base) & (lane < base + 4)
                packed = jnp.where(inside, pltpu.roll(value, base + 2, 1), packed)
        pk[stage] = packed

    pack(buf1, 0)
    zs1 = z_copies(0, 6)

    @pl.when(jnp.logical_not(bottom))
    def _():
        zs1[0].start()

    @pl.when(jnp.logical_not(top))
    def _():
        zs1[1].start()

    if n_z > 2:
        @pl.when(me[2] < n_z - 2)
        def _():
            pl.semaphore_wait(chain, 1)

        @pl.when((me[2] > 0) & (me[2] < n_z - 1))
        def _():
            pl.semaphore_signal(chain, inc=1, device_id=down[2], device_id_type=MESH)

    @pl.when(bottom)
    def _():
        zs1[0].start()

    limit = jnp.where(me[2] == 0, CUTZ, 0)
    for x in range(X):
        v = vol[x]
        fl = flg[x]
        weight = jnp.sum(jnp.where(lane < CUTZ, v, 0.0), axis=1, keepdims=True)
        excess = jnp.where((fl == 1) & (lane < limit), 1.0 - v, 0.0)
        scale[x] = jnp.where(fl != 2, 1.0 / jnp.maximum(v, VOLUME_FLOOR), 0.0)
        keep[x] = excess
        gain[x] = jnp.where(lane < limit, v / weight, 0.0)

    def boundary_z(stage):
        own = pk[stage]
        still = jnp.where(quad == 0, pltpu.roll(own, Z - 2, 1), pltpu.roll(own, Z - 1, 1))
        low = jnp.where(bottom, still, rec_low[stage])
        high = rec_high[0] if stage == 0 else jnp.where(top, rec_high[0], rec_high[stage])
        lefts, rights, slopes = [], [], []
        for c in (jnp.where(quad < 2, own, high), jnp.where(quad < 2, low, own)):
            d = c - pltpu.roll(c, 1, 1)
            s = minmod(d, pltpu.roll(d, Z - 1, 1))
            slopes.append(s)
            lefts.append(c + 0.5 * s)
            rights.append(c - 0.5 * s)
        first_lane = quad == 0
        left = jnp.where(first_lane, pltpu.roll(lefts[0], Z - 1, 1), lefts[1])
        right = jnp.where(
            first_lane, pltpu.roll(rights[0], Z - 2, 1), pltpu.roll(rights[1], Z - 1, 1)
        )
        sfix[...] = jnp.where(
            first_lane, pltpu.roll(slopes[0], Z - 1, 1), pltpu.roll(slopes[1], Z - 1, 1)
        )
        opening = jnp.where(
            first_lane, pltpu.roll(high, Z - 2, 1), pltpu.roll(own, Z - 1, 1)
        )
        ls = [pltpu.roll(left, Z - f * F4, 1) if f else left for f in range(NF)]
        rs = [pltpu.roll(right, Z - f * F4, 1) if f else right for f in range(NF)]
        opening = pltpu.roll(opening, Z - NF * F4, 1)
        live = lane < F4
        ls = [jnp.where(live & (quad < 2), w, 1.0) for w in ls]
        rs = [jnp.where(live & (quad < 2), w, 1.0) for w in rs]
        g = face(ls, rs, 3, 0.5 * opening)
        for f in range(NF):
            gfix[f] = g[f]
        afix[...] = opening

    def local_part(x, buf):
        v = [buf[f, x + 2, PAD:PAD + Y, :] for f in range(NF)]
        press[x] = pressure_of(v, 1.0 / v[0])
        for f in range(NF):
            d = v[f] - pltpu.roll(v[f], 1, 1)
            inner[f, x] = minmod(d, pltpu.roll(d, Z - 1, 1))

    def z_part(x, buf):
        v = [buf[f, x + 2, PAD:PAD + Y, :] for f in range(NF)]
        p = press[x]
        a = oz[x]
        shift = Z - (4 * x + 1)
        sl = []
        for f in range(NF):
            s = inner[f, x]
            fix = pltpu.roll(sfix[...], lax.rem(2 * Z - (f * F4 + 4 * x + 1), Z), 1)
            sl.append(0.5 * jnp.where((lane == 0) | (lane == Z - 1), fix, s))
        left = [pltpu.roll(v[f] + sl[f], 1, 1) for f in range(NF)]
        right = [v[f] - sl[f] for f in range(NF)]
        g = face(left, right, 3, 0.5 * a)
        div = [acc[f, x] for f in range(NF)]
        for f in range(NF):
            fix = pltpu.roll(gfix[f], shift, 1)
            low = jnp.where(lane == 0, fix, g[f])
            high = jnp.where(lane == Z - 1, fix, pltpu.roll(g[f], Z - 1, 1))
            div[f] = div[f] + (high - low)
        a_high = jnp.where(
            lane == Z - 1, pltpu.roll(afix[...], shift, 1), pltpu.roll(a, Z - 1, 1)
        )
        div[3] = div[3] - p * (a_high - a)
        for f in range(NF):
            acc[f, x] = div[f]

    def y_part(x, buf):
        p = press[x]
        E = Y + 8
        left, right, div = [], [], []
        for f in range(NF):
            c = buf[f, x + 2, PAD - 1:PAD - 1 + E, :]
            b = buf[f, x + 2, PAD - 2:PAD - 2 + E, :]
            n = buf[f, x + 2, PAD:PAD + E, :]
            s = 0.5 * minmod(c - b, n - c)
            left.append(c + s)
            right.append(pltpu.roll(c - s, E - 1, 0))
        a = oy[x]
        g = face(left, right, 2, 0.5 * a)
        for f in range(NF):
            div.append(pltpu.roll(g[f], E - 1, 0)[:Y] - g[f][:Y])
        div[2] = div[2] - p * (oy[x, 1:Y + 1, :] - oy[x, 0:Y, :])
        for f in range(NF):
            acc[f, x] = div[f]

    def x_part(buf, finish):
        def load(f, x):
            return buf[f, x + 2, PAD:PAD + Y, :]

        def half_slope(x):
            return [
                0.5 * minmod(load(f, x) - load(f, x - 1), load(f, x + 1) - load(f, x))
                for f in range(NF)
            ]

        s = half_slope(-1)
        left = [load(f, -1) + s[f] for f in range(NF)]
        below = None
        for x in range(X + 1):
            s = half_slope(x)
            right = [load(f, x) - s[f] for f in range(NF)]
            g = face(left, right, 1, 0.5 * ox[x])
            left = [load(f, x) + s[f] for f in range(NF)]
            if x > 0:
                c = x - 1
                rates = []
                for f in range(NF):
                    total = acc[f, c] + (g[f] - below[f])
                    if f == 1:
                        total = total - press[c] * (ox[x] - ox[c])
                    base = -total * scale[c]
                    moved = jnp.sum(keep[c] * base, axis=1, keepdims=True)
                    rates.append((1.0 - keep[c]) * base + gain[c] * moved)
                finish(c, rates)
            below = g

    def loop(part, buf):
        def body(x, carry):
            part(x, buf)
            return carry

        lax.fori_loop(0, X, body, 0, unroll=True)

    def arrive(copies):
        for c in copies:
            c.wait_recv()

    loop(local_part, buf1)
    arrive(ys1 + (ay,))
    loop(y_part, buf1)
    zs1[0].wait_recv()

    @pl.when(jnp.logical_not(bottom))
    def _():
        zs1[1].wait_recv()

    boundary_z(0)
    loop(z_part, buf1)
    arrive((ax,) + xs1)

    xs2 = x_copies(buf2, 2, rows, buf2, 8)
    ys2 = y_copies(buf2, 2, PAD, buf2, 10)
    zs2 = z_copies(1, 12)

    def finish_first(c, rates):
        for f in range(NF):
            first[f, c] = rates[f]
            buf2[f, c + 2, PAD:PAD + Y, :] = buf1[f, c + 2, PAD:PAD + Y, :] + TIME_STEP * rates[f]
        if c == 1:
            xs2[0].start()
        if c == X - 1:
            xs2[1].start()

    x_part(buf1, finish_first)
    for c in ys2:
        c.start()
    pack(buf2, 1)

    @pl.when(jnp.logical_not(bottom))
    def _():
        zs2[0].start()

    @pl.when(jnp.logical_not(top))
    def _():
        zs2[1].start()

    loop(local_part, buf2)
    arrive(ys2)
    loop(y_part, buf2)

    @pl.when(jnp.logical_not(top))
    def _():
        zs2[0].wait_recv()

    @pl.when(jnp.logical_not(bottom))
    def _():
        zs2[1].wait_recv()

    boundary_z(1)
    loop(z_part, buf2)
    arrive(xs2)

    def finish_second(c, rates):
        for f in range(NF):
            out[f, c] = 0.5 * (first[f, c] + rates[f])

    x_part(buf2, finish_second)
    for c in xs1 + ys1 + (ax, ay, zs1[0]) + xs2 + ys2:
        c.wait_send()

    @pl.when(jnp.logical_not(top))
    def _():
        zs1[1].wait_send()
        zs2[1].wait_send()

    @pl.when(jnp.logical_not(bottom))
    def _():
        zs2[0].wait_send()


def on_device(state, volume, apertures, flags):
    _, X, Y, Z = state.shape
    f32 = jnp.float32
    wide = pltpu.VMEM((NF, X + 4, Y + 2 * PAD, Z), f32)
    cells = pltpu.VMEM((X, Y, Z), f32)
    fields = pltpu.VMEM((NF, X, Y, Z), f32)
    layer = pltpu.VMEM((Y, Z), f32)
    pair = pltpu.VMEM((2, Y, Z), f32)
    return pl.pallas_call(
        kernel,
        out_shape=pltpu.VMEM(state.shape, f32),
        in_specs=[pl.BlockSpec(memory_space=pl.ANY)] * 4,
        out_specs=pl.BlockSpec(memory_space=pltpu.VMEM),
        scratch_shapes=[
            wide, wide,
            pltpu.VMEM((X + 1, Y, Z), f32),
            pltpu.VMEM((X, Y + 8, Z), f32),
            cells, cells, pltpu.VMEM((X, Y, Z), jnp.int32),
            pair, pair, pair,
            pltpu.VMEM((NF, Y, Z), f32), layer, layer,
            fields, fields, cells, cells, cells,
            pltpu.SemaphoreType.DMA((6,)),
            pltpu.SemaphoreType.DMA((14,)),
            pltpu.SemaphoreType.DMA((14,)),
            pltpu.SemaphoreType.REGULAR,
            cells, fields,
        ],
        compiler_params=pltpu.CompilerParams(collective_id=0, has_side_effects=True),
    )(state, volume, apertures, flags)


def solution(mesh):
    in_specs = (
        P(None, "gx", "gy", "gz"),
        P("gx", "gy", "gz"),
        P(None, "gx", "gy", "gz"),
        P("gx", "gy", "gz"),
    )
    return jax.shard_map(
        on_device, mesh=mesh, in_specs=in_specs, out_specs=P(None, "gx", "gy", "gz"),
        check_vma=False,
    )
```
